32 devices in a mesh: row: 8 (over y, x, core), col: 4 (over z).
Axes of the slice: x: 2, y: 2, z: 4, core: 2. Of those that a mesh axis runs over, the one named last changes fastest.
Arguments:
- layer_input: bfloat16 [8192, 1536], P(('row', 'col')), may hold values from -6 to 6
- context: bfloat16 [8, 130, 768], P('row'), may hold values from -6 to 6
- first_gain: float32 [1536], replicated, may hold values from 0.5 to 1.5
- query_weight: bfloat16 [1536, 1536], P('row', 'col'), may hold values from -0.15625 to 0.15625
- key_weight: bfloat16 [1536, 1536], P('row', 'col'), may hold values from -0.15625 to 0.15625
- value_weight: bfloat16 [1536, 1536], P('row', 'col'), may hold values from -0.15625 to 0.15625
- out_weight: bfloat16 [1536, 1536], P(('col', 'row')), may hold values from -3 to 3
- second_gain: float32 [1536], replicated, may hold values from 0.5 to 1.5
- cross_query: bfloat16 [1536, 1536], P('row', 'col'), may hold values from -0.15625 to 0.15625
- cross_key: bfloat16 [768, 1536], P('row', 'col'), may hold values from -0.21875 to 0.21875
- cross_value: bfloat16 [768, 1536], P('row', 'col'), may hold values from -0.21875 to 0.21875
- cross_out: bfloat16 [1536, 1536], P(('col', 'row')), may hold values from -1 to 1
- third_gain: float32 [1536], replicated, may hold values from 0.5 to 1.5
- gate_weight: bfloat16 [1536, 6144], P('row', 'col'), may hold values from -0.15625 to 0.15625
- up_weight: bfloat16 [1536, 6144], P('row', 'col'), may hold values from -0.15625 to 0.15625
- gate_bias: float32 [6144], P('col'), may hold values from -3 to 3
- up_bias: float32 [6144], P('col'), may hold values from -3 to 3
- down_weight: bfloat16 [6144, 1536], P(('col', 'row')), may hold values from -0.078125 to 0.078125
- down_bias: float32 [1536], replicated, may hold values from -3 to 3
- out_grad: bfloat16 [8192, 1536], P(('row', 'col')), may hold values from -6 to 6
Outputs:
- output: bfloat16 [8192, 1536], P(('row', 'col'))
- input_grad: float32 [8192, 1536], P(('row', 'col'))
- context_grad: float32 [8, 130, 768], P('row')
- first_gain_grad: float32 [1536], replicated
- query_grad: float32 [1536, 1536], P('row', 'col')
- key_grad: float32 [1536, 1536], P('row', 'col')
- value_grad: float32 [1536, 1536], P('row', 'col')
- out_weight_grad: float32 [1536, 1536], P(('col', 'row'))
- second_gain_grad: float32 [1536], replicated
- cross_query_grad: float32 [1536, 1536], P('row', 'col')
- cross_key_grad: float32 [768, 1536], P('row', 'col')
- cross_value_grad: float32 [768, 1536], P('row', 'col')
- cross_out_grad: float32 [1536, 1536], P(('col', 'row'))
- third_gain_grad: float32 [1536], replicated
- gate_grad: float32 [1536, 6144], P('row', 'col')
- up_grad: float32 [1536, 6144], P('row', 'col')
- gate_bias_grad: float32 [6144], P('col')
- up_bias_grad: float32 [6144], P('col')
- down_grad: float32 [6144, 1536], P(('col', 'row'))
- down_bias_grad: float32 [1536], replicated
The draws below stay inside these ranges and needn't reach their ends.
All inputs are finite; a program needn't handle non-finite values.
Results may differ from the reference program's by a relative error of at most 0.024.
Values may be sent and summed in bfloat16 or wider, within the bound.
No kernel may reach another device: no remote copies, remote signals or barrier semaphores. Data moves between devices by JAX's collectives and lax.ppermute only.
A program may use at most 192 MiB of HBM per device.

```python
import jax
import jax.numpy as jnp
from jax import lax

D = 1536
HEADS = 24
HD = 64
FF = 6144
DC = 768
CT = 130
LEN = 1024
TOKENS = 8192
SEQS = 8


def block_levels(stream_key, shape, cuts, smallest, largest):
    level = 1.0
    for dim, shards_of in cuts:
        steps = jax.random.uniform(jax.random.fold_in(jax.random.fold_in(stream_key, 6), dim), (shards_of,), jnp.float32, smallest / len(cuts), largest / len(cuts))
        level = level * jnp.repeat(jnp.exp(steps), shape[dim] // shards_of).reshape((-1,) + (1,) * (len(shape) - 1 - dim))
    return level


def bell_draw(rng, extent, scale, most, split=(), kind=jnp.bfloat16):
    values = scale * jax.random.normal(rng, extent, jnp.float32)
    if split:
        values = values * block_levels(rng, extent, split, -0.22, 0.18)
    return jnp.clip(values, -most, most).astype(kind)


def setup_inputs(seed: int = 0) -> dict:
    key_of = jax.random.split(jax.random.key(seed), 21)
    return {
        "layer_input": bell_draw(key_of[0], (TOKENS, D), 1.0, 6.0, ((0, 32),)),
        "context": bell_draw(key_of[1], (SEQS, CT, DC), 1.0, 6.0, ((0, 8),)),
        "first_gain": jnp.clip(1.0 + 0.1 * jax.random.normal(key_of[2], (D,), jnp.float32), 0.5, 1.5),
        "query_weight": bell_draw(key_of[3], (D, D), D ** -0.5, 0.15625, ((0, 8), (1, 4))),
        "key_weight": bell_draw(key_of[4], (D, D), D ** -0.5, 0.15625, ((0, 8), (1, 4))),
        "value_weight": bell_draw(key_of[5], (D, D), D ** -0.5, 0.15625, ((0, 8), (1, 4))),
        "out_weight": bell_draw(key_of[6], (D, D), (max(1, D // 384)) ** -0.5, 3.0, ((0, 32),)),
        "second_gain": jnp.clip(1.0 + 0.1 * jax.random.normal(key_of[7], (D,), jnp.float32), 0.5, 1.5),
        "cross_query": bell_draw(key_of[8], (D, D), D ** -0.5, 0.15625, ((0, 8), (1, 4))),
        "cross_key": bell_draw(key_of[9], (DC, D), DC ** -0.5, 0.21875, ((0, 8), (1, 4))),
        "cross_value": bell_draw(key_of[10], (DC, D), DC ** -0.5, 0.21875, ((0, 8), (1, 4))),
        "cross_out": bell_draw(key_of[11], (D, D), (max(1, D // 48)) ** -0.5, 1.0, ((0, 32),)),
        "third_gain": jnp.clip(1.0 + 0.1 * jax.random.normal(key_of[12], (D,), jnp.float32), 0.5, 1.5),
        "gate_weight": bell_draw(key_of[13], (D, FF), D ** -0.5, 0.15625, ((0, 8), (1, 4))),
        "up_weight": bell_draw(key_of[14], (D, FF), D ** -0.5, 0.15625, ((0, 8), (1, 4))),
        "gate_bias": bell_draw(key_of[15], (FF,), 0.5, 3.0, ((0, 4),), jnp.float32),
        "up_bias": bell_draw(key_of[16], (FF,), 0.5, 3.0, ((0, 4),), jnp.float32),
        "down_weight": bell_draw(key_of[17], (FF, D), FF ** -0.5, 0.078125, ((0, 32),)),
        "down_bias": bell_draw(key_of[18], (D,), 0.5, 3.0, (), jnp.float32),
        "out_grad": bell_draw(key_of[19], (TOKENS, D), 1.0, 6.0, ((0, 32),)),
    }


@jax.custom_vjp
def low(v):
    return lax.optimization_barrier(v.astype(jnp.bfloat16)).astype(jnp.float32)

@jax.custom_vjp
def low_back(v):
    return v

def low_keep(v):
    return (low(v), None)

def low_pass(kept, grad):
    return (grad,)

def back_keep(v):
    return (v, None)

def back_low(kept, grad):
    return (low(grad),)
low.defvjp(low_keep, low_pass)
low_back.defvjp(back_keep, back_low)
norm_eps = 1e-05
highest = lax.Precision.HIGHEST

def product(left, right):
    return jnp.dot(left, right, precision=highest)

def layer_norm(stream, gain):
    average = lax.optimization_barrier(jnp.mean(stream, axis=-1, keepdims=True))
    centred = stream - average
    spread = lax.optimization_barrier(jnp.mean(centred * centred, axis=-1, keepdims=True))
    return centred * lax.rsqrt(spread + norm_eps) * gain

def rotary(values):
    quarter = HD // 4
    freqs = 10000.0 ** (-jnp.arange(quarter, dtype=jnp.float32) / quarter)
    places = jnp.arange(LEN, dtype=jnp.int32).astype(jnp.float32)
    angles = places[:, None] * freqs[None, :]
    cosine = jnp.cos(angles)[:, None, :]
    sine = jnp.sin(angles)[:, None, :]
    first = values[..., :quarter]
    second = values[..., quarter:2 * quarter]
    return jnp.concatenate([first * cosine - 1.0 * second * sine, second * cosine + 1.0 * first * sine, values[..., 2 * quarter:]], axis=-1)

def attend(triple):
    queries, keys, values = triple
    scores = low_back(jnp.einsum('qhd,khd->hqk', queries, keys, precision=highest) * HD ** (-0.5))
    probs = low(jax.nn.softmax(scores, axis=-1))
    return jnp.einsum('hqk,khd->qhd', probs, values, precision=highest)

def forward(layer_input, context, first_gain, query_weight, key_weight, value_weight, out_weight, second_gain, cross_query, cross_key, cross_value, cross_out, third_gain, gate_weight, up_weight, gate_bias, up_bias, down_weight, down_bias):
    seq_count = layer_input.shape[0] // LEN
    shaped = (seq_count, LEN, HEADS, HD)
    ctx_shape = (seq_count, CT, HEADS, HD)
    acts_one = low(layer_norm(layer_input, first_gain))
    queries = low(rotary(low_back(product(acts_one, query_weight)).reshape(shaped)))
    keys = low(rotary(low_back(product(acts_one, key_weight)).reshape(shaped)))
    values = low(low_back(product(acts_one, value_weight))).reshape(shaped)
    attended = lax.map(jax.checkpoint(attend), (queries, keys, values)).reshape(-1, HEADS * HD)
    mixed_self = low(low_back(attended))
    stream_one = layer_input + low_back(product(mixed_self, out_weight))
    acts_two = low(layer_norm(stream_one, second_gain))
    other_queries = low(low_back(product(acts_two, cross_query))).reshape(shaped)
    other_keys = low(low_back(jnp.einsum('sce,ef->scf', context, cross_key, precision=highest))).reshape(ctx_shape)
    other_values = low(low_back(jnp.einsum('sce,ef->scf', context, cross_value, precision=highest))).reshape(ctx_shape)
    other_att = lax.map(jax.checkpoint(attend), (other_queries, other_keys, other_values)).reshape(-1, HEADS * HD)
    mixed_other = low(low_back(other_att))
    stream_two = stream_one + low_back(product(mixed_other, cross_out))
    acts_three = low(layer_norm(stream_two, third_gain))
    gate = low_back(product(acts_three, gate_weight) + gate_bias)
    upward = low_back(product(acts_three, up_weight) + up_bias)
    hidden = low(jax.nn.silu(gate) * upward)
    return stream_two + low_back(product(hidden, down_weight) + down_bias)

def reference(layer_input, context, first_gain, query_weight, key_weight, value_weight, out_weight, second_gain, cross_query, cross_key, cross_value, cross_out, third_gain, gate_weight, up_weight, gate_bias, up_bias, down_weight, down_bias, out_grad):
    primals = (layer_input.astype(jnp.float32), context.astype(jnp.float32), first_gain, query_weight.astype(jnp.float32), key_weight.astype(jnp.float32), value_weight.astype(jnp.float32), out_weight.astype(jnp.float32), second_gain, cross_query.astype(jnp.float32), cross_key.astype(jnp.float32), cross_value.astype(jnp.float32), cross_out.astype(jnp.float32), third_gain, gate_weight.astype(jnp.float32), up_weight.astype(jnp.float32), gate_bias, up_bias, down_weight.astype(jnp.float32), down_bias)
    result, pullback = jax.vjp(forward, *primals)
    grads = pullback(out_grad.astype(jnp.float32))
    return (result.astype(jnp.bfloat16), grads[0], grads[1], grads[2], grads[3], grads[4], grads[5], grads[6], grads[7], grads[8], grads[9], grads[10], grads[11], grads[12], grads[13], grads[14], grads[15], grads[16], grads[17], grads[18])
```

```python
import jax
import jax.numpy as jnp
from jax import lax
from jax.sharding import PartitionSpec as P


HD = 64
norm_eps = 1e-05
bf16 = jnp.bfloat16
f32 = jnp.float32


def mixed(left, right):
    return jnp.dot(left, right, preferred_element_type=f32)


def mixed_t(left, right):
    return lax.dot_general(left, right, (((1,), (1,)), ((), ())), preferred_element_type=f32)


def outer(left, right):
    return lax.dot_general(left, right, (((0,), (0,)), ((), ())), preferred_element_type=f32)


def norm_forward(stream):
    average = jnp.mean(stream, axis=1, keepdims=True)
    centred = stream - average
    spread = jnp.mean(centred * centred, axis=1, keepdims=True)
    inverse = lax.rsqrt(spread + norm_eps)
    return (centred * inverse, inverse)


def norm_backward(grad_normed, normed, inverse, gain):
    scaled = grad_normed * gain
    first_mean = jnp.mean(scaled, axis=1, keepdims=True)
    second_mean = jnp.mean(scaled * normed, axis=1, keepdims=True)
    grad_stream = inverse * (scaled - first_mean - normed * second_mean)
    return (grad_stream, jnp.sum(grad_normed * normed, axis=0))


def rotate(values, cosine, sine, direction):
    quarter = cosine.shape[-1]
    first = values[..., :quarter]
    second = values[..., quarter : 2 * quarter]
    return jnp.concatenate(
        [
            first * cosine - direction * second * sine,
            second * cosine + direction * first * sine,
            values[..., 2 * quarter :],
        ],
        axis=-1,
    )


def attend(query, key, value, scale):
    scores = jnp.einsum("qhd,khd->hqk", query, key, preferred_element_type=f32) * scale
    row_peak = jnp.max(scores, axis=-1, keepdims=True)
    lifted = jnp.exp(scores - row_peak)
    totals = jnp.sum(lifted, axis=-1, keepdims=True)
    probs = (lifted / totals).astype(bf16)
    result = jnp.einsum("hqk,khd->qhd", probs, value, preferred_element_type=f32)
    return (result.astype(bf16), (row_peak + jnp.log(totals))[..., 0])


def attend_back(query, key, value, grad_block, block_sum, scale):
    scores = jnp.einsum("qhd,khd->hqk", query, key, preferred_element_type=f32) * scale
    probs = jnp.exp(scores - block_sum[..., None])
    grad_probs = jnp.einsum("qhd,khd->hqk", grad_block, value, preferred_element_type=f32)
    weighted = jnp.sum(grad_probs * probs, axis=-1, keepdims=True)
    grad_scores = (probs * (grad_probs - weighted)).astype(bf16)
    grad_query = jnp.einsum("hqk,khd->qhd", grad_scores, key, preferred_element_type=f32) * scale
    grad_key = jnp.einsum("hqk,qhd->khd", grad_scores, query, preferred_element_type=f32) * scale
    grad_value = jnp.einsum(
        "hqk,qhd->khd", probs.astype(bf16), grad_block, preferred_element_type=f32
    )
    return (grad_query, grad_key, grad_value)


def after(value, *others):
    return lax.optimization_barrier((value,) + others)[0]


def column_sums(value):
    ones = lax.optimization_barrier(jnp.full((8, value.shape[0]), 0.125, bf16))
    return jnp.sum(mixed(ones, value), axis=0)


class Line:
    def __init__(self):
        self.mark = ()

    def take(self, *values):
        out = lax.optimization_barrier(tuple(values) + self.mark)[: len(values)]
        return out[0] if len(values) == 1 else out

    def leave(self, *values):
        self.mark = tuple(values)


def make_local(rows, cols):
    ranks = range(cols)
    pairs = rows // 2

    def swap(value, slot):
        return lax.ppermute(value, "col", [(i, i ^ slot) for i in ranks])

    def swap_row(value, slot):
        return lax.ppermute(value, "row", [(i, i ^ slot) for i in range(rows)])

    def spread(value):
        return [value] + [swap(value, k) for k in ranks[1:]]

    def send_back(parts):
        return [parts[0]] + [swap(parts[k].astype(bf16), k) for k in ranks[1:]]

    def add_up(pieces):
        total = pieces[0].astype(f32)
        for piece in pieces[1:]:
            total = total + piece.astype(f32)
        return total

    def reorder(blocks):
        me = lax.axis_index("col")
        stacked = jnp.stack(blocks)
        return [
            lax.dynamic_index_in_dim(stacked, jnp.bitwise_xor(me, j), 0, keepdims=False)
            for j in ranks
        ]

    def sum_over(value, axis, size):
        step = 1
        while step < size:
            hops = [(i, i ^ step) for i in range(size)]
            value = value + lax.ppermute(value, axis, hops)
            step *= 2
        return value

    def widen(value):
        return lax.all_gather(value, "col", axis=0, tiled=True)

    def narrow(value):
        return lax.psum_scatter(value, "col", scatter_dimension=0, tiled=True)

    def gather_one(value):
        return [value] + [swap_row(value, 2 * k) for k in range(1, pairs)]

    def gather_two(received):
        mine = jnp.stack(received)
        return mine, swap_row(mine, 1)

    def gather_three(mine, other, shape, pick=lambda block: block, axis=0):
        row = lax.axis_index("row")
        pair, side = row // 2, row % 2
        out = jnp.zeros(shape, mine.dtype)
        for half, at in ((mine, side), (other, 1 - side)):
            for k in range(pairs):
                block = jnp.expand_dims(pick(half[k]), axis)
                start = [0] * len(shape)
                start[axis] = 2 * jnp.bitwise_xor(pair, k) + at
                out = lax.dynamic_update_slice(out, block, tuple(start))
        return out

    def scatter_one(value):
        side = lax.axis_index("row") % 2
        halves = value.reshape((pairs, 2) + value.shape[1:])
        mine = lax.dynamic_index_in_dim(halves, side, 1, keepdims=False)
        other = lax.dynamic_index_in_dim(halves, 1 - side, 1, keepdims=False)
        return mine, swap_row(other, 1)

    def scatter_two(mine, received):
        half = (mine.astype(f32) + received.astype(f32)).astype(bf16)
        pair = lax.axis_index("row") // 2

        def block(k):
            return lax.dynamic_index_in_dim(half, jnp.bitwise_xor(pair, k), 0, keepdims=False)

        return [block(0)] + [swap_row(block(k), 2 * k) for k in range(1, pairs)]

    def local(
        layer_input,
        context,
        first_gain,
        query_weight,
        key_weight,
        value_weight,
        out_weight,
        second_gain,
        cross_query,
        cross_key,
        cross_value,
        cross_out,
        third_gain,
        gate_weight,
        up_weight,
        gate_bias,
        up_bias,
        down_weight,
        down_bias,
        out_grad,
    ):
        me = lax.axis_index("col")
        width = query_weight.shape[1]
        heads = width // HD
        all_heads = heads * cols
        features = layer_input.shape[1]
        own = layer_input.shape[0]
        tokens = own * cols
        ctx = context[0]
        ctx_len, _ = ctx.shape
        hidden_width = gate_weight.shape[1]
        scale = HD ** (-0.5)
        cq_rows, co_rows = cross_query.shape[0], cross_out.shape[0]
        line = Line()

        def block_of(value, j):
            return lax.slice_in_dim(value, j * own, (j + 1) * own, axis=0)

        def slot_of(value, k):
            return lax.dynamic_slice_in_dim(value, jnp.bitwise_xor(me, k) * own, own, axis=0)

        stream = layer_input.astype(f32)
        normed_one, inverse_one = norm_forward(stream)
        acts_one = (normed_one * first_gain).astype(bf16)
        qkv_shard = jnp.concatenate([query_weight, key_weight, value_weight], axis=1)
        ckv_weight = jnp.concatenate([cross_key, cross_value], axis=1)
        mix_shard = jnp.concatenate([out_weight, ckv_weight.reshape(-1, features)], axis=0)
        gu_shard = jnp.concatenate([gate_weight, up_weight], axis=1)
        cross_shard = jnp.concatenate([cross_query.reshape(-1, features), cross_out], axis=0)
        acts_wide = widen(acts_one)
        qkv_one = gather_one(qkv_shard)
        line.leave(acts_one)
        qkv_two = gather_two(line.take(*qkv_one))
        line.leave(qkv_two[0])
        mix_one = gather_one(line.take(mix_shard))
        gu_one = gather_one(after(line.take(gu_shard), mix_one[1]))
        qkv_cols = gather_three(*line.take(*qkv_two), (rows,) + qkv_shard.shape)
        qkv_cols = qkv_cols.reshape(features, -1)
        line.leave(qkv_cols)
        mix_two = gather_two(line.take(*mix_one))
        line.leave(mix_two[0])
        mix_two = line.take(*mix_two)
        shape = (rows, co_rows, features)
        out_rows = gather_three(*mix_two, shape, lambda block: block[:co_rows])
        out_rows = out_rows.reshape(-1, features)
        shape = (rows, mix_shard.shape[0] - co_rows, features)
        ckv_cols = gather_three(*mix_two, shape, lambda block: block[co_rows:])
        ckv_cols = ckv_cols.reshape(-1, ckv_weight.shape[1])
        ckv = mixed(ctx, ckv_cols).astype(bf16)
        line.leave(ckv, out_rows, ckv_cols)
        ckv_got = spread(ckv)

        quarter = HD // 4
        freqs = 10000.0 ** (-jnp.arange(quarter, dtype=f32) / quarter)
        angles = jnp.arange(tokens, dtype=jnp.int32).astype(f32)[:, None] * freqs[None, :]
        cosine, sine = jnp.cos(angles)[:, None, :], jnp.sin(angles)[:, None, :]
        acts_wide, cosine, sine = line.take(acts_wide, cosine, sine)
        cross_got = spread(after(cross_shard, acts_wide))
        grads_wide = widen(after(out_grad, acts_wide))
        qkv = mixed(acts_wide, qkv_cols)
        split = [qkv[:, j * width : (j + 1) * width].reshape(tokens, heads, HD) for j in range(3)]
        queries = rotate(split[0], cosine, sine, 1.0).astype(bf16)
        keys = rotate(split[1], cosine, sine, 1.0).astype(bf16)
        values = split[2].astype(bf16)
        line.leave(queries, keys, values)
        queries, keys, values = line.take(queries, keys, values)
        results = [None] * cols

        def attend_blocks(js):
            for j in js:
                results[j] = attend(line.take(block_of(queries, j)), keys, values, scale)
                line.leave(*results[j])

        half = cols // 2
        attend_blocks(range(half))
        shards = reorder(line.take(*cross_got))
        cq_shard = jnp.concatenate(
            [shard[:-co_rows].reshape(cq_rows, width) for shard in shards], axis=1
        )
        cross_all = jnp.concatenate([cq_shard] + [shard[-co_rows:] for shard in shards], axis=0)
        line.leave(cross_all)
        cross_one = gather_one(cross_all)
        attend_blocks(range(half, cols))
        self_mixed = jnp.concatenate([r[0] for r in results], axis=0).reshape(tokens, width)
        self_sum = [r[1] for r in results]
        out_value = mixed(line.take(self_mixed), out_rows).astype(bf16)
        line.leave(out_value)
        settled_one = narrow(out_value)

        gu_two = gather_two(line.take(*gu_one))
        line.leave(gu_two[0])
        cross_two = gather_two(line.take(*cross_one))
        line.leave(cross_two[0])
        down_one = gather_one(line.take(down_weight))
        blocks = reorder(line.take(*ckv_got))
        other_keys = jnp.concatenate([b[:, :width] for b in blocks], axis=1)
        other_values = jnp.concatenate([b[:, width:] for b in blocks], axis=1)
        other_keys = other_keys.reshape(ctx_len, all_heads, HD)
        other_values = other_values.reshape(ctx_len, all_heads, HD)
        line.leave(other_keys, other_values)
        cross_two = line.take(*cross_two)
        shape = (rows, cq_rows, features)
        cq_full = gather_three(*cross_two, shape, lambda block: block[:cq_rows])
        cq_full = cq_full.reshape(features, features)
        shape = (cols, rows, co_rows, features)

        def pick(block):
            return block[cq_rows:].reshape(cols, co_rows, features)

        co_full = gather_three(*cross_two, shape, pick, 1).reshape(features, features)
        line.leave(cq_full, co_full)
        gu_cols = gather_three(*line.take(*gu_two), (rows,) + gu_shard.shape)
        gu_cols = gu_cols.reshape(features, -1)
        line.leave(gu_cols)

        stream_one = stream + line.take(settled_one).astype(f32)
        normed_two, inverse_two = norm_forward(stream_one)
        acts_two = (normed_two * second_gain).astype(bf16)
        other_queries = mixed(acts_two, cq_full).astype(bf16).reshape(own, all_heads, HD)
        other_mixed, other_sum = attend(other_queries, other_keys, other_values, scale)
        other_flat = other_mixed.reshape(own, features)
        stream_two = stream_one + mixed(other_flat, co_full)
        normed_three, inverse_three = norm_forward(stream_two)
        acts_three = (normed_three * third_gain).astype(bf16)
        line.leave(acts_three)
        acts_three = widen(acts_three)
        down_two = gather_two(line.take(*down_one))
        line.leave(down_two[0])
        down_rows = gather_three(*line.take(*down_two), (rows,) + down_weight.shape)
        down_rows = down_rows.reshape(-1, features)
        line.leave(down_rows)

        acts_three, grads_wide = line.take(acts_three, grads_wide)
        parts = [None] * cols
        all_hidden = jnp.zeros((tokens, hidden_width), bf16)
        all_grad_gu = jnp.zeros((tokens, 2 * hidden_width), bf16)
        for k in ranks[::-1]:
            acts, grad_slot = line.take(slot_of(acts_three, k), slot_of(grads_wide, k))
            gu = mixed(acts, gu_cols)
            gate = gu[:, :hidden_width] + gate_bias
            upward = gu[:, hidden_width:] + up_bias
            sigmoid_gate = jax.nn.sigmoid(gate)
            silu_gate = gate * sigmoid_gate
            hidden = (silu_gate * upward).astype(bf16)
            grad_hidden = mixed_t(grad_slot, down_rows)
            grad_up = (grad_hidden * silu_gate).astype(bf16)
            grad_gate = (
                grad_hidden * upward * sigmoid_gate * (1.0 + gate * (1.0 - sigmoid_gate))
            ).astype(bf16)
            grad_gu = line.take(jnp.concatenate([grad_gate, grad_up], axis=1))
            parts[k] = mixed_t(grad_gu, gu_cols).astype(bf16)
            line.leave(parts[k])
            here = (jnp.bitwise_xor(me, k) * own, 0)
            all_hidden = lax.dynamic_update_slice(all_hidden, hidden, here)
            all_grad_gu = lax.dynamic_update_slice(all_grad_gu, grad_gu, here)
        three_got = send_back(parts)
        gu_part = outer(acts_three, line.take(all_grad_gu)).astype(bf16)
        line.leave(gu_part)
        gu_one = scatter_one(gu_part.reshape(rows, -1, gu_part.shape[-1]))
        down_part = outer(line.take(all_hidden), grads_wide).astype(bf16)
        line.leave(down_part)
        down_back = scatter_one(down_part.reshape(rows, -1, features))
        down_value = mixed(line.take(all_hidden), down_rows).astype(bf16)
        line.leave(down_value)
        settled_down = narrow(down_value)
        gu_two = scatter_two(*line.take(*gu_one))
        line.leave(gu_two[0])
        down_two = scatter_two(*line.take(*down_back))
        line.leave(down_two[0])

        grad_acts_three = add_up(line.take(*three_got))
        grad_norm_three, third_gain_part = norm_backward(
            grad_acts_three, normed_three, inverse_three, third_gain
        )
        grad_two = out_grad.astype(f32) + grad_norm_three
        grad_two_low = grad_two.astype(bf16)
        grad_other = mixed_t(grad_two_low, co_full).astype(bf16)
        grad_oq, grad_ok, grad_ov = attend_back(
            other_queries,
            other_keys,
            other_values,
            grad_other.reshape(own, all_heads, HD),
            other_sum,
            scale,
        )
        grad_oq = grad_oq.astype(bf16).reshape(own, features)
        grad_acts_two = mixed_t(grad_oq, cq_full)
        grad_norm_two, second_gain_part = norm_backward(
            grad_acts_two, normed_two, inverse_two, second_gain
        )
        grad_one = grad_two + grad_norm_two
        grad_one_low = grad_one.astype(bf16)
        line.leave(grad_one_low, grad_ok, grad_ov)
        grad_one_wide = widen(grad_one_low)

        grad_oq, grad_two_low = line.take(grad_oq, grad_two_low)
        cq_part = outer(acts_two, grad_oq).astype(bf16)
        co_part = outer(other_flat, grad_two_low).astype(bf16)
        co_part = co_part.reshape(cols, rows, -1, features)
        co_part = jnp.moveaxis(co_part, 0, 1).reshape(rows, -1, features)
        cross_part = jnp.concatenate([cq_part.reshape(rows, -1, features), co_part], axis=1)
        line.leave(cross_part)
        cross_back = scatter_one(cross_part)
        gu_bias = column_sums(line.take(all_grad_gu))
        down_bias_part = column_sums(out_grad)
        line.leave(gu_bias, down_bias_part)
        cross_two = scatter_two(*line.take(*cross_back))
        line.leave(cross_two[0])

        def blocks_of(value):
            return [value[:, j * width : (j + 1) * width] for j in ranks]

        grad_one_wide = line.take(grad_one_wide)
        kv_blocks = [
            jnp.concatenate([x, y], axis=1).astype(bf16)
            for x, y in zip(
                blocks_of(grad_ok.reshape(ctx_len, features)),
                blocks_of(grad_ov.reshape(ctx_len, features)),
            )
        ]
        kv_blocks = reorder([after(b, grad_one_wide) for b in kv_blocks])
        kv_got = send_back(kv_blocks)
        grad_self = mixed_t(grad_one_wide, out_rows).astype(bf16).reshape(tokens, heads, HD)
        grad_query, grad_keys, grad_values = [None] * cols, None, None

        def back_blocks(js):
            nonlocal grad_keys, grad_values
            for j in js:
                grad_query[j], gk, gv = attend_back(
                    line.take(block_of(queries, j)),
                    keys,
                    values,
                    block_of(grad_self, j),
                    self_sum[j],
                    scale,
                )
                grad_keys = gk if grad_keys is None else grad_keys + gk
                grad_values = gv if grad_values is None else grad_values + gv
                line.leave(grad_query[j], grad_keys, grad_values)

        back_blocks(range(half))
        grad_ckv = add_up(line.take(*kv_got)).astype(bf16)
        context_part = mixed_t(grad_ckv, ckv_cols).astype(bf16)
        ckv_part = outer(ctx, grad_ckv).astype(bf16)
        line.leave(context_part, ckv_part)
        context_got = spread(context_part)
        back_blocks(range(half, cols))
        grad_query, grad_keys, grad_values = line.take(
            jnp.concatenate(grad_query, axis=0), grad_keys, grad_values
        )
        gq = rotate(grad_query, cosine, sine, -1.0).astype(bf16)
        gk = rotate(grad_keys, cosine, sine, -1.0).astype(bf16)
        gv = grad_values.astype(bf16)
        grad_qkv = jnp.concatenate([v.reshape(tokens, width) for v in (gq, gk, gv)], axis=1)
        part = mixed_t(grad_qkv, qkv_cols).astype(bf16)
        line.leave(part, grad_qkv)
        settled_last = narrow(part)

        qkv_part = outer(acts_wide, line.take(grad_qkv)).astype(bf16)
        line.leave(qkv_part)
        qkv_back = scatter_one(qkv_part.reshape(rows, -1, 3 * width))
        out_part = outer(line.take(self_mixed), grad_one_wide).astype(bf16)
        small_part = jnp.concatenate(
            [out_part.reshape(rows, -1, features), ckv_part.reshape(rows, -1, features)],
            axis=1,
        )
        line.leave(small_part)
        small_back = scatter_one(small_part)
        qkv_two = scatter_two(*line.take(*qkv_back))
        line.leave(qkv_two[0])
        small_two = scatter_two(*line.take(*small_back))
        line.leave(small_two[0])
        cross_half = add_up(line.take(*cross_two)).astype(bf16)
        cq_blocks = blocks_of(cross_half[:cq_rows])
        co_blocks = cross_half[cq_rows:].reshape(cols, co_rows, features)
        cross_blocks = [
            jnp.concatenate([cq_blocks[j].reshape(-1, features), co_blocks[j]], axis=0)
            for j in ranks
        ]
        cross_blocks = reorder(cross_blocks)
        line.leave(*cross_blocks)
        cross_got = send_back(cross_blocks)
        gu_grad = add_up(line.take(*gu_two))
        down_grad = add_up(line.take(*down_two))
        first_gain_part = jnp.sum(part.astype(f32) * acts_wide.astype(f32), axis=0) / first_gain
        sums = jnp.concatenate(
            [first_gain_part, second_gain_part, third_gain_part, down_bias_part, gu_bias]
        )
        line.leave(sums, gu_grad, down_grad)
        sums = sum_over(line.take(sums), "row", rows)
        line.leave(sums)
        qkv_grad = add_up(line.take(*qkv_two))
        small_grad = add_up(line.take(*small_two))
        output_value = (stream_two + line.take(settled_down).astype(f32) + down_bias).astype(bf16)
        line.leave(qkv_grad, small_grad, output_value)

        settled_last, sums = line.take(settled_last, sums)
        gains, gu_bias = sums[: 4 * features], sums[4 * features :]
        gains = sum_over(gains, "col", cols).reshape(4, features)
        grad_norm_one, _ = norm_backward(
            settled_last.astype(f32), normed_one, inverse_one, first_gain
        )
        input_grad = grad_one + grad_norm_one
        context_grad = add_up(reorder(line.take(*context_got)))
        cross_grad = add_up(line.take(*cross_got))
        cross_query_grad = cross_grad[:-co_rows].reshape(cq_rows, width)
        cross_out_grad = cross_grad[-co_rows:]
        ckv_grad = small_grad[co_rows:].reshape(-1, 2 * width)
        return (
            output_value,
            input_grad,
            context_grad[None],
            gains[0],
            qkv_grad[:, :width],
            qkv_grad[:, width : 2 * width],
            qkv_grad[:, 2 * width :],
            small_grad[:co_rows],
            gains[1],
            cross_query_grad,
            ckv_grad[:, :width],
            ckv_grad[:, width:],
            cross_out_grad,
            gains[2],
            gu_grad[:, :hidden_width],
            gu_grad[:, hidden_width:],
            gu_bias[:hidden_width],
            gu_bias[hidden_width:],
            down_grad,
            gains[3],
        )

    return local


def solution(mesh):
    row_col = P("row", "col")
    tokens = P(("row", "col"), None)
    tall = P(("col", "row"), None)
    seqs = P("row", None, None)
    in_specs = (
        tokens,
        seqs,
        P(),
        row_col,
        row_col,
        row_col,
        tall,
        P(),
        row_col,
        row_col,
        row_col,
        tall,
        P(),
        row_col,
        row_col,
        P("col"),
        P("col"),
        tall,
        P(),
        tokens,
    )
    out_specs = (
        tokens,
        tokens,
        seqs,
        P(),
        row_col,
        row_col,
        row_col,
        tall,
        P(),
        row_col,
        row_col,
        row_col,
        tall,
        P(),
        row_col,
        row_col,
        P("col"),
        P("col"),
        tall,
        P(),
    )
    local = make_local(mesh.shape["row"], mesh.shape["col"])

    return jax.shard_map(local, mesh=mesh, in_specs=in_specs, out_specs=out_specs, check_vma=False)
```
